256 devices in a mesh: dp: 16 (over y, x_lo, core), tensor: 16 (over x_hi, z).
Axes of the slice: x: 4 (x_hi: 2, x_lo: 2; x = x_hi * 2 + x_lo), y: 4, z: 8, core: 2. Of those that a mesh axis runs over, the one named last changes fastest.
Arguments:
- gate_pre: bfloat16 [28, 512, 16384], P(None, 'tensor', 'dp'), parts along dimension 2, may hold values from -6 to 6
- up_pre: bfloat16 [28, 512, 16384], P(None, 'tensor', 'dp'), parts along dimension 2, may hold values from -6 to 6
- down_weight: bfloat16 [28, 512, 4096], P(None, 'tensor'), may hold values from -0.0625 to 0.0625
Outputs:
- mixed: bfloat16 [4096, 16384], P('tensor', 'dp'), parts along dimension 1
The draws below stay inside these ranges and needn't reach their ends.
There are 16 independent parts, one for each index of `dp`. The reference program is written for one: setup_inputs(seed, part) draws one part's arguments, and reference() takes and returns one part's arrays. A program takes and returns all parts, laid end to end along the dimension named above; an argument that names none is the same for every part. Nothing has to cross between parts.
All inputs are finite; a program needn't handle non-finite values.
Results may differ from the reference program's by a relative error of at most 0.024.
Values may be sent and summed in bfloat16 or wider, within the bound.
A program may use at most 128 MiB of HBM per device.

```python
import math
import jax
import jax.numpy as jnp
import numpy as np
from jax import lax

HF = 28
HB = 512
DOUT = 4096
TOK = 1024
FF = 14336
N_TENSOR = 16


def strengthened(values, stream_key, source, target, blocks, factor):
    def block_of(axis_at):
        return (jnp.arange(values.shape[axis_at]) // (values.shape[axis_at] // blocks)).reshape((-1,) + (1,) * (values.ndim - 1 - axis_at))

    near = jax.random.permutation(stream_key, blocks)[block_of(target)]
    far = (block_of(target) + blocks // 2) % blocks
    return jnp.where((block_of(source) == near) | (block_of(source) == far), factor * values, values)


def levels(rng, shape, pieces, least, high):
    factor_of, own = 1.0, jax.random.fold_in(rng, 6)
    for axis_at, parts in pieces:
        steps = jnp.exp(jax.random.uniform(jax.random.fold_in(own, axis_at), (parts,), jnp.float32, least / len(pieces), high / len(pieces)))
        factor_of = factor_of * jnp.repeat(steps, shape[axis_at] // parts).reshape([-1 if axis == axis_at else 1 for axis in range(len(shape))])
    return factor_of


def scatter_about(rng, dims, deviation, most, split=(), dtype=jnp.bfloat16):
    result = deviation * jax.random.normal(rng, dims, jnp.float32)
    if split:
        result = result * levels(rng, dims, split, -0.22, 0.18)
    return jnp.clip(result, -most, most).astype(dtype)


def bell_draw_with(key, extent, deviation, bound, split, heavy, held_as=jnp.bfloat16):
    drawn = deviation * jax.random.normal(key, extent, jnp.float32)
    if split:
        drawn = drawn * levels(key, extent, split, -0.22, 0.18)
    return jnp.clip(strengthened(drawn, jax.random.fold_in(key, 3), *heavy), -bound, bound).astype(held_as)


def setup_inputs(seed: int = 0, part: int = 0) -> dict:
    seeds = jax.random.split(jax.random.key(seed), 4)
    part_splits = jax.random.split(jax.random.fold_in(seeds[3], part), 4)
    gate_pre = scatter_about(part_splits[0], (HF, HB, TOK), 1.0, 6.0, ((1, 16),))
    up_pre = scatter_about(part_splits[1], (HF, HB, TOK), 1.0, 6.0, ((1, 16),))
    down_weight = bell_draw_with(seeds[2], (HF, HB, DOUT), FF ** -0.5, 0.0625, ((1, 16),), (1, 2, 16, 2.0))
    return dict(gate_pre=gate_pre, up_pre=up_pre, down_weight=down_weight)


def character(value, prime_order):
    residue = value % prime_order
    if residue == 0:
        return 0
    squares_list = [index * index % prime_order for index in range(1, prime_order)]
    return 1 if residue in squares_list else -1

def paley_matrix():
    prime_order = 13
    conference = np.zeros((14, 14))
    conference[0, 1:] = 1.0
    conference[1:, 0] = 1.0
    for row_index in range(prime_order):
        for col_index in range(prime_order):
            conference[row_index + 1, col_index + 1] = character(col_index - row_index, prime_order)
    first = np.array([[1.0, 1.0], [1.0, -1.0]])
    second = np.array([[1.0, -1.0], [-1.0, -1.0]])
    return np.kron(conference, first) + np.kron(np.eye(14), second)

def sylvester(order):
    matrix = np.ones((1, 1))
    basic = np.array([[1.0, 1.0], [1.0, -1.0]])
    while matrix.shape[0] < order:
        matrix = np.kron(basic, matrix)
    return matrix

def reference(gate_pre, up_pre, down_weight):
    hidden = (jax.nn.silu(gate_pre.astype(jnp.float32)) * up_pre.astype(jnp.float32)).astype(jnp.bfloat16)
    left_factor = jnp.asarray(paley_matrix(), jnp.float32)
    right_factor = jnp.asarray(sylvester(HB), jnp.float32)
    transformed = jnp.einsum('ij,jbt->ibt', left_factor, hidden.astype(jnp.float32), precision=lax.Precision.DEFAULT)
    transformed = jnp.einsum('bc,act->abt', right_factor, transformed, precision=lax.Precision.HIGH)
    rotated = (transformed * (1.0 / math.sqrt(HF * HB))).astype(jnp.bfloat16)
    group_width = HB // N_TENSOR
    total = jnp.zeros((DOUT, TOK), jnp.float32)
    for block_index in range(N_TENSOR):
        rot_rows = rotated[:, block_index * group_width:(block_index + 1) * group_width, :].reshape(HF * group_width, TOK)
        weight_rows = down_weight[:, block_index * group_width:(block_index + 1) * group_width, :].reshape(HF * group_width, DOUT)
        partial_value = lax.dot_general(weight_rows, rot_rows, (((0,), (0,)), ((), ())), preferred_element_type=jnp.float32)
        partial_value = lax.optimization_barrier(partial_value.astype(jnp.bfloat16)).astype(jnp.float32)
        total = total + partial_value
    return total.astype(jnp.bfloat16)
```

```python
import functools
import math

import jax
import jax.numpy as jnp
import numpy as np
from jax import lax
from jax.experimental import pallas as pl
from jax.experimental.pallas import tpu as pltpu
from jax.sharding import PartitionSpec as P

MESH = pl.DeviceIdType.MESH
BF = jnp.bfloat16
F32 = jnp.float32

NZ = 8
KL = 896
KB = 112
TOKENS = 1024
TH = 512
TQ = 256
CW = 128


def character(value, prime_order):
    residue = value % prime_order
    if residue == 0:
        return 0
    squares_list = [index * index % prime_order for index in range(1, prime_order)]
    return 1 if residue in squares_list else -1


def paley_matrix():
    prime_order = 13
    conference = np.zeros((14, 14))
    conference[0, 1:] = 1.0
    conference[1:, 0] = 1.0
    for row_index in range(prime_order):
        for col_index in range(prime_order):
            conference[row_index + 1, col_index + 1] = character(col_index - row_index, prime_order)
    first = np.array([[1.0, 1.0], [1.0, -1.0]])
    second = np.array([[1.0, -1.0], [-1.0, -1.0]])
    return np.kron(conference, first) + np.kron(np.eye(14), second)


def sylvester(order):
    matrix = np.ones((1, 1))
    basic = np.array([[1.0, 1.0], [1.0, -1.0]])
    while matrix.shape[0] < order:
        matrix = np.kron(basic, matrix)
    return matrix


def place(d):
    d %= NZ
    return max(0, 2 * (4 - d) - 1) if d <= 4 else 2 * (d - 4)


GROUPS = ((0, 3), (3, 2), (5, 3))
NG = len(GROUPS)
CHAINS = (("a+", 0, 1, 4), ("b-", 1, -1, 4), ("b+", 1, 1, 3), ("a-", 0, -1, 3))


def kernel(scale, gate, up, weight, hmat, out,
           gbuf, ubuf, hbuf, hid, rot, rec1, snd2, stg, wbuf, part, rsend, rrecv,
           load_sem, p1s, p1r, p2s, p2r, xs, xr, ys, yr, cs, cr, hs, hr, rs, rr):
    dp = lax.axis_index("dp")
    tn = lax.axis_index("tensor")
    y = dp // 4
    xl = lax.rem(dp // 2, 2)
    core = lax.rem(dp, 2)
    xh = tn // NZ
    z = lax.rem(tn, NZ)
    block = y * 2 + xl
    crossed = core != xh

    def dev(y_=None, xl_=None, core_=None, xh_=None, z_=None):
        y_ = y if y_ is None else y_
        xl_ = xl if xl_ is None else xl_
        core_ = core if core_ is None else core_
        xh_ = xh if xh_ is None else xh_
        z_ = z if z_ is None else z_
        return (y_ * 4 + xl_ * 2 + core_, xh_ * NZ + z_)

    def zat(o):
        return lax.rem(z + (o % NZ), NZ)

    def yat(o):
        return lax.rem(y + (o % 4), 4)

    def remote(src, dst, s, r, to):
        return pltpu.make_async_remote_copy(
            src_ref=src, dst_ref=dst, send_sem=s, recv_sem=r, device_id=to, device_id_type=MESH)

    sent = []

    def send(src, dst, s, r, to):
        c = remote(src, dst, s, r, to)
        c.start()
        sent.append(c)

    def recv(dst, s, r, frm):
        remote(dst, dst, s, r, frm).wait_recv()

    loads = []
    for t in range(2):
        ts = pl.ds(t * TH, TH)
        for i, (src, dst) in enumerate(((gate, gbuf), (up, ubuf))):
            c = pltpu.make_async_copy(src.at[:, ts], dst.at[:, ts], load_sem.at[t * 2 + i])
            c.start()
            loads.append(c)
    c = pltpu.make_async_copy(hmat, hbuf, load_sem.at[4])
    c.start()
    loads.append(c)

    barrier = pltpu.get_barrier_semaphore()
    partners = [dev(z_=zat(o)) for o in range(1, NZ)]
    partners += [dev(y_=yat(1)), dev(y_=yat(-1)), dev(core_=1 - core), dev(xh_=1 - xh)]
    partners += [dev(xl_=1 - xl, core_=xh, xh_=core)]
    for to in partners:
        pl.semaphore_signal(barrier, inc=1, device_id=to, device_id_type=MESH)

    @pl.when(crossed)
    def _():
        pl.semaphore_signal(barrier, inc=1, device_id=dev(core_=xh, xh_=core), device_id_type=MESH)
        pl.semaphore_wait(barrier, len(partners) + 1)

    @pl.when(jnp.logical_not(crossed))
    def _():
        pl.semaphore_wait(barrier, len(partners))

    rows1 = pl.ds(pl.multiple_of(block * KB, 16), KB)

    def cols1(j, zz):
        return pl.ds(pl.multiple_of(core * (NZ * 2 * CW) + zz * (2 * CW) + j * CW, 128), CW)

    def p1_send(j):
        for o in range(1, NZ):
            zz = zat(o)
            send(weight.at[rows1, cols1(j, zz)], rec1.at[j, z], p1s.at[j, o], p1r.at[j, o], dev(z_=zz))
        pltpu.make_async_copy(weight.at[rows1, cols1(j, z)], rec1.at[j, z], p1r.at[j, 0]).start()

    def p1_wait_rotate(j):
        pltpu.make_async_copy(weight.at[rows1, cols1(j, z)], rec1.at[j, z], p1r.at[j, 0]).wait()
        for o in range(1, NZ):
            zz = zat(-o)
            recv(rec1.at[j, zz], p1s.at[j, o], p1r.at[j, o], dev(z_=zz))
        v = [rec1[j, i].astype(F32) for i in range(NZ)]
        for bit in (1, 2, 4):
            v = [v[i] + v[i ^ bit] if not i & bit else v[i ^ bit] - v[i] for i in range(NZ)]
        for i in range(NZ):
            snd2[j, i] = v[i].astype(BF)

    def p2_send(j):
        for o in range(1, NZ):
            zz = zat(o)
            send(snd2.at[j, zz], stg.at[j, :, pl.ds(place(-o) * CW, CW)], p2s.at[j, o], p2r.at[j, o], dev(z_=zz))
        stg[j, :, pl.ds(place(0) * CW, CW)] = snd2[j, z]

    def gcols(g):
        return pl.ds(GROUPS[g][0] * CW, GROUPS[g][1] * CW)

    def wrows(s, b, n):
        return pl.ds(pl.multiple_of(s * KL + b * KB, 16), n)

    def x_copy(j, g, dst_xl, i):
        return remote(stg.at[j, :, gcols(g)], wbuf.at[j, wrows(xh, block, KB), gcols(g)],
                      xs.at[j, g, i], xr.at[j, g, i], dev(xl_=dst_xl, core_=xh, xh_=core))

    def p2_wait(j):
        for o in range(1, NZ):
            recv(stg.at[j, :, pl.ds(place(-o) * CW, CW)], p2s.at[j, o], p2r.at[j, o], dev(z_=zat(-o)))

    def x_send(j, g):
        c = x_copy(j, g, 1 - xl, 1)
        c.start()
        sent.append(c)

        @pl.when(crossed)
        def _():
            x_copy(j, g, xl, 0).start()

        @pl.when(jnp.logical_not(crossed))
        def _():
            pltpu.make_async_copy(stg.at[j, :, gcols(g)], wbuf.at[j, wrows(xh, block, KB), gcols(g)],
                                  xr.at[j, g, 0]).start()

    def x_finish(j, g):
        @pl.when(crossed)
        def _():
            x_copy(j, g, xl, 0).wait_send()

    def wblock(j, g, s, yy, n=2 * KB, off=0):
        return wbuf.at[j, wrows(s, yy * 2 + off, n), gcols(g)]

    def core_fwd(j, g, yy, i):
        ref = wblock(j, g, core, yy)
        send(ref, ref, cs.at[j, g, i], cr.at[j, g, i], dev(core_=1 - core))

    def y_own(j, g):
        own = wbuf.at[j, wrows(core, block, KB), gcols(g)]
        recv(own, xs.at[j, g, 0], xr.at[j, g, 0], dev(core_=xh, xh_=core))
        other = wbuf.at[j, wrows(core, y * 2 + 1 - xl, KB), gcols(g)]
        recv(other, xs.at[j, g, 1], xr.at[j, g, 1], dev(xl_=1 - xl, core_=xh, xh_=core))
        ref = wblock(j, g, core, y)
        send(ref, ref, ys.at[j, g, 0], yr.at[j, g, 0], dev(y_=yat(1)))
        send(ref, ref, ys.at[j, g, 1], yr.at[j, g, 1], dev(y_=yat(-1)))
        core_fwd(j, g, y, 0)

    def y_near(j, g):
        for i, step in ((0, 1), (1, -1)):
            frm = yat(-step)
            recv(wblock(j, g, core, frm), ys.at[j, g, i], yr.at[j, g, i], dev(y_=frm))
            half = wblock(j, g, core, frm, KB, i)
            send(half, half, ys.at[j, g, 2 + i], yr.at[j, g, 2 + i], dev(y_=yat(step)))
            core_fwd(j, g, frm, 1 + i)

    def y_far(j, g):
        far = yat(2)
        for i, step in ((0, 1), (1, -1)):
            recv(wblock(j, g, core, far, KB, i), ys.at[j, g, 2 + i], yr.at[j, g, 2 + i], dev(y_=yat(-step)))
        core_fwd(j, g, far, 3)

    def c_wait(j, g):
        for i, o in enumerate((0, -1, 1, 2)):
            recv(wblock(j, g, 1 - core, yat(o)), cs.at[j, g, i], cr.at[j, g, i], dev(core_=1 - core))

    def silu(t):
        loads[2 * t].wait()
        loads[2 * t + 1].wait()

        def step(i, carry):
            rows = pl.ds(pl.multiple_of(i * 128, 128), 128)
            cols = pl.ds(t * TH, TH)
            half = gbuf[rows, cols].astype(F32) * 0.5
            value = (half + half * jnp.tanh(half)) * ubuf[rows, cols].astype(F32)
            hid[xh, cols, rows] = value.astype(BF).T
            return carry

        lax.fori_loop(0, KL // 128, step, 0)

    def h_ref(t, s):
        return hid.at[s, pl.ds(t * TH, TH)]

    def h_send(t):
        send(h_ref(t, xh), h_ref(t, xh), hs.at[t], hr.at[t], dev(xh_=1 - xh))

    def rotate(t):
        if t == 0:
            loads[4].wait()
        recv(h_ref(t, 1 - xh), hs.at[t], hr.at[t], dev(xh_=1 - xh))
        rows = pl.ds(t * TH, TH)
        for n0, n in ((0, 256), (256, 256), (512, 256), (768, 128)):
            m = hbuf[:, n0:n0 + n]
            l0 = jnp.dot(hid[0, rows], m, preferred_element_type=F32)
            l1 = jnp.dot(hid[1, rows], m, preferred_element_type=F32)
            rot[rows, n0:n0 + n] = ((l0 + l1) * scale).astype(BF)
            rot[rows, KL + n0:KL + n0 + n] = ((l0 - l1) * scale).astype(BF)

    def partial(p, j, t, g):
        first, n = GROUPS[g]
        for i in range(0, n, 2):
            w = min(2, n - i) * CW
            c0 = (first + i) * CW
            part[p % 2, :, c0:c0 + w] = jnp.dot(
                rot[pl.ds(t * TH, TH)], wbuf[j, :, c0:c0 + w], preferred_element_type=F32)

    def own_part(p, half, m):
        c0 = place(m) * CW
        return part[p % 2, half * TQ:(half + 1) * TQ, c0:c0 + CW]

    def rs_wait(p, k, m):
        _, half, d, _ = CHAINS[k]
        recv(rrecv.at[p, k, m], rs.at[p, k, m], rr.at[p, k, m], dev(z_=zat(-d)))
        return rrecv[p, k, m].astype(F32)

    def rs_hop(p, k, m):
        _, half, d, first = CHAINS[k]
        value = own_part(p, half, d * m)
        if m < first:
            value = value + rs_wait(p, k, m)
        rsend[p, k, m - 1] = value.astype(BF)
        send(rsend.at[p, k, m - 1], rrecv.at[p, k, m - 1], rs.at[p, k, m - 1], rr.at[p, k, m - 1],
             dev(z_=zat(d)))

    def rs_step(p, s):
        for k in range(4):
            m = CHAINS[k][3] - s
            if m >= 1:
                rs_hop(p, k, m)

    def rs_final(p, j, t):
        for half, (ka, kb) in ((0, (3, 0)), (1, (2, 1))):
            value = own_part(p, half, 0) + rs_wait(p, ka, 0) + rs_wait(p, kb, 0)
            c0 = t * TH + half * TQ
            out[j * CW:(j + 1) * CW, c0:c0 + TQ] = value.T.astype(BF)

    p1_send(0)
    p1_send(1)
    silu(0)
    h_send(0)
    p1_wait_rotate(0)
    p2_send(0)
    silu(1)
    p1_wait_rotate(1)
    p2_send(1)
    p2_wait(0)
    for g in range(NG):
        x_send(0, g)
    h_send(1)
    for g in range(NG):
        y_own(0, g)
    y_near(0, 0)
    p2_wait(1)
    for g in range(NG):
        x_send(1, g)
    y_far(0, 0)
    y_near(0, 1)
    rotate(0)
    c_wait(0, 0)
    partial(0, 0, 0, 0)
    rs_step(0, 0)
    y_far(0, 1)
    y_near(0, 2)
    for g in range(NG):
        y_own(1, g)
    c_wait(0, 1)
    partial(0, 0, 0, 1)
    rs_step(0, 1)
    y_far(0, 2)
    c_wait(0, 2)
    partial(0, 0, 0, 2)
    rs_step(0, 2)
    y_near(1, 0)
    rs_step(0, 3)
    y_far(1, 0)
    rotate(1)
    for g in range(NG):
        partial(1, 0, 1, g)
    rs_step(1, 0)
    y_near(1, 1)
    rs_final(0, 0, 0)
    rs_step(1, 1)
    y_far(1, 1)
    y_near(1, 2)
    c_wait(1, 0)
    partial(2, 1, 0, 0)
    rs_step(2, 0)
    rs_step(1, 2)
    y_far(1, 2)
    c_wait(1, 1)
    partial(2, 1, 0, 1)
    rs_step(1, 3)
    rs_step(2, 1)
    c_wait(1, 2)
    partial(2, 1, 0, 2)
    rs_final(1, 0, 1)
    rs_step(2, 2)
    for g in range(NG):
        partial(3, 1, 1, g)
    rs_step(3, 0)
    rs_step(2, 3)
    rs_step(3, 1)
    rs_final(2, 1, 0)
    rs_step(3, 2)
    rs_step(3, 3)
    rs_final(3, 1, 1)

    for c in sent:
        c.wait_send()
    for j in range(2):
        for g in range(NG):
            x_finish(j, g)


def body(gate_pre, up_pre, down_weight):
    hmat = jnp.asarray(np.kron(paley_matrix(), sylvester(32)), BF)
    dma = pltpu.SemaphoreType.DMA
    any_spec = pl.BlockSpec(memory_space=pl.ANY)
    return pl.pallas_call(
        functools.partial(kernel, 1.0 / math.sqrt(16 * KL)),
        out_shape=jax.ShapeDtypeStruct((2 * CW, TOKENS), BF),
        in_specs=[any_spec] * 4,
        out_specs=pl.BlockSpec(memory_space=pltpu.VMEM),
        scratch_shapes=[
            pltpu.VMEM((KL, TOKENS), BF),
            pltpu.VMEM((KL, TOKENS), BF),
            pltpu.VMEM((KL, KL), BF),
            pltpu.VMEM((2, TOKENS, KL), BF),
            pltpu.VMEM((TOKENS, 2 * KL), BF),
            pltpu.VMEM((2, NZ, KB, CW), BF),
            pltpu.VMEM((2, NZ, KB, CW), BF),
            pltpu.VMEM((2, KB, NZ * CW), BF),
            pltpu.VMEM((2, 2 * KL, NZ * CW), BF),
            pltpu.VMEM((2, TH, NZ * CW), F32),
            pltpu.VMEM((4, 4, 4, TQ, CW), BF),
            pltpu.VMEM((4, 4, 4, TQ, CW), BF),
            dma((5,)),
            dma((2, NZ)), dma((2, NZ)),
            dma((2, NZ)), dma((2, NZ)),
            dma((2, NG, 2)), dma((2, NG, 2)),
            dma((2, NG, 4)), dma((2, NG, 4)),
            dma((2, NG, 4)), dma((2, NG, 4)),
            dma((2,)), dma((2,)),
            dma((4, 4, 4)), dma((4, 4, 4)),
        ],
        compiler_params=pltpu.CompilerParams(
            collective_id=0, has_side_effects=True, vmem_limit_bytes=56 << 20),
        name="rotated_down_projection",
    )(gate_pre.reshape(KL, TOKENS), up_pre.reshape(KL, TOKENS),
      down_weight.reshape(KL, 16 * 2 * CW), hmat)


def solution(mesh):
    in_specs = (P(None, "tensor", "dp"), P(None, "tensor", "dp"), P(None, "tensor", None))
    out_specs = P("tensor", "dp")
    return jax.shard_map(body, mesh=mesh, in_specs=in_specs, out_specs=out_specs, check_vma=False)
```

```python
import functools
import math

import jax
import jax.numpy as jnp
import numpy as np
from jax import lax
from jax.experimental import pallas as pl
from jax.experimental.pallas import tpu as pltpu
from jax.sharding import PartitionSpec as P

MESH = pl.DeviceIdType.MESH
BF = jnp.bfloat16
F32 = jnp.float32

NZ = 8
KL = 896
KB = 112
TOKENS = 1024
TH = 512
TQ = 256
NQ = TOKENS // TQ
HX = 64
CW = 128


def character(value, prime_order):
    residue = value % prime_order
    if residue == 0:
        return 0
    squares_list = [index * index % prime_order for index in range(1, prime_order)]
    return 1 if residue in squares_list else -1


def paley_matrix():
    prime_order = 13
    conference = np.zeros((14, 14))
    conference[0, 1:] = 1.0
    conference[1:, 0] = 1.0
    for row_index in range(prime_order):
        for col_index in range(prime_order):
            conference[row_index + 1, col_index + 1] = character(col_index - row_index, prime_order)
    first = np.array([[1.0, 1.0], [1.0, -1.0]])
    second = np.array([[1.0, -1.0], [-1.0, -1.0]])
    return np.kron(conference, first) + np.kron(np.eye(14), second)


def sylvester(order):
    matrix = np.ones((1, 1))
    basic = np.array([[1.0, 1.0], [1.0, -1.0]])
    while matrix.shape[0] < order:
        matrix = np.kron(basic, matrix)
    return matrix


def place(d):
    d %= NZ
    return max(0, 2 * (4 - d) - 1) if d <= 4 else 2 * (d - 4)


GROUPS = ((0, 1), (1, 2), (3, 2), (5, 3))
NG = len(GROUPS)


def chain(q, k):
    return (1, 4 - q % 2) if k == 0 else (-1, 3 + q % 2)


NAME = "rotated_down_projection"


def kernel(scale, gate, up, weight, hmat, out,
           gbuf, ubuf, hbuf, hid, rot, rec1, snd2, stg, wbuf, part, rsend, rrecv,
           load_sem, p1s, p1r, p2s, p2r, xs, xr, ys, yr, cs, cr, hs, hr, rs, rr):
    dp = lax.axis_index("dp")
    tn = lax.axis_index("tensor")
    y = dp // 4
    xl = lax.rem(dp // 2, 2)
    core = lax.rem(dp, 2)
    xh = tn // NZ
    z = lax.rem(tn, NZ)
    block = y * 2 + xl
    crossed = core != xh

    def dev(y_=None, xl_=None, core_=None, xh_=None, z_=None):
        y_ = y if y_ is None else y_
        xl_ = xl if xl_ is None else xl_
        core_ = core if core_ is None else core_
        xh_ = xh if xh_ is None else xh_
        z_ = z if z_ is None else z_
        return (y_ * 4 + xl_ * 2 + core_, xh_ * NZ + z_)

    def zat(o):
        return lax.rem(z + (o % NZ), NZ)

    def yat(o):
        return lax.rem(y + (o % 4), 4)

    def remote(src, dst, s, r, to):
        return pltpu.make_async_remote_copy(
            src_ref=src, dst_ref=dst, send_sem=s, recv_sem=r, device_id=to, device_id_type=MESH)

    sent = []

    def send(src, dst, s, r, to):
        c = remote(src, dst, s, r, to)
        c.start()
        sent.append(c)

    def recv(dst, s, r, frm):
        remote(dst, dst, s, r, frm).wait_recv()

    loads = []

    def load(src, dst):
        c = pltpu.make_async_copy(src, dst, load_sem.at[len(loads)])
        c.start()
        loads.append(c)

    def load_all():
        for t in range(2):
            ts = pl.ds(t * TH, TH)
            load(gate.at[:, ts], gbuf.at[:, ts])
            load(up.at[:, ts], ubuf.at[:, ts])
        load(hmat, hbuf)

    barrier = pltpu.get_barrier_semaphore()
    partners = [dev(z_=zat(o)) for o in range(1, NZ)]
    partners += [dev(y_=yat(1)), dev(y_=yat(-1)), dev(core_=1 - core), dev(xh_=1 - xh)]
    partners += [dev(xl_=1 - xl, core_=xh, xh_=core)]
    for to in partners:
        pl.semaphore_signal(barrier, inc=1, device_id=to, device_id_type=MESH)

    @pl.when(crossed)
    def _():
        pl.semaphore_signal(barrier, inc=1, device_id=dev(core_=xh, xh_=core), device_id_type=MESH)

    def meet():
        @pl.when(crossed)
        def _():
            pl.semaphore_wait(barrier, len(partners) + 1)

        @pl.when(jnp.logical_not(crossed))
        def _():
            pl.semaphore_wait(barrier, len(partners))

    rows1 = pl.ds(pl.multiple_of(block * KB, 16), KB)

    def cols1(j, zz):
        return pl.ds(pl.multiple_of(core * (NZ * 2 * CW) + zz * (2 * CW) + j * CW, 128), CW)

    def p1_send(j):
        for o in range(1, NZ):
            zz = zat(o)
            send(weight.at[rows1, cols1(j, zz)], rec1.at[j, z], p1s.at[j, o], p1r.at[j, o], dev(z_=zz))
        pltpu.make_async_copy(weight.at[rows1, cols1(j, z)], rec1.at[j, z], p1r.at[j, 0]).start()

    def p1_wait_rotate(j):
        pltpu.make_async_copy(weight.at[rows1, cols1(j, z)], rec1.at[j, z], p1r.at[j, 0]).wait()
        for o in range(1, NZ):
            zz = zat(-o)
            recv(rec1.at[j, zz], p1s.at[j, o], p1r.at[j, o], dev(z_=zz))
        v = [rec1[j, i].astype(F32) for i in range(NZ)]
        for bit in (1, 2, 4):
            v = [v[i] + v[i ^ bit] if not i & bit else v[i ^ bit] - v[i] for i in range(NZ)]
        for i in range(NZ):
            snd2[j, i] = v[i].astype(BF)

    def p2_send(j):
        for o in sorted(range(1, NZ), key=lambda o: place(-o)):
            zz = zat(o)
            send(snd2.at[j, zz], stg.at[j, :, pl.ds(place(-o) * CW, CW)], p2s.at[j, o], p2r.at[j, o], dev(z_=zz))
        stg[j, :, pl.ds(place(0) * CW, CW)] = snd2[j, z]

    def gcols(g):
        return pl.ds(GROUPS[g][0] * CW, GROUPS[g][1] * CW)

    def wrows(s, b, n):
        return pl.ds(pl.multiple_of(s * KL + b * KB, 16), n)

    def x_copy(j, g, dst_xl, i):
        return remote(stg.at[j, :, gcols(g)], wbuf.at[j, wrows(xh, block, KB), gcols(g)],
                      xs.at[j, g, i], xr.at[j, g, i], dev(xl_=dst_xl, core_=xh, xh_=core))

    crossing = []

    def x_send(j, g):
        crossing.append((j, g))
        for o in range(1, NZ):
            if 0 <= place(-o) - GROUPS[g][0] < GROUPS[g][1]:
                recv(stg.at[j, :, pl.ds(place(-o) * CW, CW)], p2s.at[j, o], p2r.at[j, o], dev(z_=zat(-o)))
        c = x_copy(j, g, 1 - xl, 1)
        c.start()
        sent.append(c)

        @pl.when(crossed)
        def _():
            x_copy(j, g, xl, 0).start()

        @pl.when(jnp.logical_not(crossed))
        def _():
            pltpu.make_async_copy(stg.at[j, :, gcols(g)], wbuf.at[j, wrows(xh, block, KB), gcols(g)],
                                  xr.at[j, g, 0]).start()

    def x_finish(j, g):
        @pl.when(crossed)
        def _():
            x_copy(j, g, xl, 0).wait_send()

    def wblock(j, g, s, yy, n=2 * KB, off=0):
        return wbuf.at[j, wrows(s, yy * 2 + off, n), gcols(g)]

    def core_fwd(j, g, yy, i):
        ref = wblock(j, g, core, yy)
        send(ref, ref, cs.at[j, g, i], cr.at[j, g, i], dev(core_=1 - core))

    def y_own(j, g):
        own = wbuf.at[j, wrows(core, block, KB), gcols(g)]
        recv(own, xs.at[j, g, 0], xr.at[j, g, 0], dev(core_=xh, xh_=core))
        other = wbuf.at[j, wrows(core, y * 2 + 1 - xl, KB), gcols(g)]
        recv(other, xs.at[j, g, 1], xr.at[j, g, 1], dev(xl_=1 - xl, core_=xh, xh_=core))
        ref = wblock(j, g, core, y)
        send(ref, ref, ys.at[j, g, 0], yr.at[j, g, 0], dev(y_=yat(1)))
        send(ref, ref, ys.at[j, g, 1], yr.at[j, g, 1], dev(y_=yat(-1)))
        core_fwd(j, g, y, 0)

    def y_near(j, g, i):
        step = 1 - 2 * i
        frm = yat(-step)
        recv(wblock(j, g, core, frm), ys.at[j, g, i], yr.at[j, g, i], dev(y_=frm))
        half = wblock(j, g, core, frm, KB, i)
        send(half, half, ys.at[j, g, 2 + i], yr.at[j, g, 2 + i], dev(y_=yat(step)))
        core_fwd(j, g, frm, 1 + i)

    def y_far(j, g):
        far = yat(2)
        for i, step in ((0, 1), (1, -1)):
            recv(wblock(j, g, core, far, KB, i), ys.at[j, g, 2 + i], yr.at[j, g, 2 + i], dev(y_=yat(-step)))
        core_fwd(j, g, far, 3)

    def w_wait(j, g):
        for i, o in enumerate((0, -1, 1, 2)):
            recv(wblock(j, g, 1 - core, yat(o)), cs.at[j, g, i], cr.at[j, g, i], dev(core_=1 - core))

    def silu(t):
        loads[2 * t].wait()
        loads[2 * t + 1].wait()

        def step(i, carry):
            rows = pl.ds(pl.multiple_of(i * 128, 128), 128)
            cols = pl.ds(t * TH, TH)
            half = gbuf[rows, cols].astype(F32) * 0.5
            value = (half + half * jnp.tanh(half)) * ubuf[rows, cols].astype(F32)
            hid[xh, cols, rows] = value.astype(BF).T
            return carry

        lax.fori_loop(0, KL // 128, step, 0)

    def h_ref(q, s):
        return hid.at[s, pl.ds(q * HX, HX)]

    def h_send(q):
        send(h_ref(q, xh), h_ref(q, xh), hs.at[q], hr.at[q], dev(xh_=1 - xh))

    def rotate(q):
        if not rotated:
            loads[4].wait()
        rotated.add(q)
        for i in range(q * TQ // HX, (q + 1) * TQ // HX):
            recv(h_ref(i, 1 - xh), hs.at[i], hr.at[i], dev(xh_=1 - xh))
        rows = pl.ds(q * TQ, TQ)
        for n0, n in ((0, 256), (256, 256), (512, 256), (768, 128)):
            m = hbuf[:, n0:n0 + n]
            l0 = jnp.dot(hid[0, rows], m, preferred_element_type=F32)
            l1 = jnp.dot(hid[1, rows], m, preferred_element_type=F32)
            rot[rows, n0:n0 + n] = ((l0 + l1) * scale).astype(BF)
            rot[rows, KL + n0:KL + n0 + n] = ((l0 - l1) * scale).astype(BF)

    rotated = set()
    complete = set()

    def partial(j, q, g):
        if (j, g) not in complete:
            w_wait(j, g)
            complete.add((j, g))
        first, n = GROUPS[g]
        for i in range(0, n, 2):
            w = min(2, n - i) * CW
            c0 = (first + i) * CW
            part[j, pl.ds(q * TQ, TQ), c0:c0 + w] = jnp.dot(
                rot[pl.ds(q * TQ, TQ)], wbuf[j, :, c0:c0 + w], preferred_element_type=F32)

    def own_part(j, q, m):
        c0 = place(m) * CW
        return part[j, pl.ds(q * TQ, TQ), c0:c0 + CW]

    def rs_wait(j, q, k, m):
        p = j * NQ + q
        recv(rrecv.at[p, k, m], rs.at[p, k, m], rr.at[p, k, m], dev(z_=zat(-chain(q, k)[0])))
        return rrecv[p, k, m].astype(F32)

    def rs_hop(j, q, k, m):
        p = j * NQ + q
        d, first = chain(q, k)
        value = own_part(j, q, d * m)
        if m < first:
            value = value + rs_wait(j, q, k, m)
        rsend[p, k, m - 1] = value.astype(BF)
        send(rsend.at[p, k, m - 1], rrecv.at[p, k, m - 1], rs.at[p, k, m - 1], rr.at[p, k, m - 1],
             dev(z_=zat(d)))

    def rs_final(j, q):
        value = own_part(j, q, 0) + rs_wait(j, q, 0, 0) + rs_wait(j, q, 1, 0)
        out[j * CW:(j + 1) * CW, q * TQ:(q + 1) * TQ] = value.T.astype(BF)

    load_all()
    silu(0)
    silu(1)
    meet()
    p1_send(0)
    p1_send(1)
    h_send(0)
    h_send(1)
    h_send(2)
    h_send(3)
    p1_wait_rotate(0)
    p2_send(0)
    h_send(4)
    h_send(5)
    p1_wait_rotate(1)
    p2_send(1)
    x_send(0, 0)
    h_send(6)
    rotate(0)
    x_send(0, 1)
    h_send(7)
    x_send(0, 2)
    x_send(0, 3)
    h_send(8)
    x_send(1, 0)
    y_own(0, 0)
    x_send(1, 1)
    h_send(9)
    x_send(1, 2)
    y_near(0, 0, 0)
    y_near(0, 0, 1)
    y_own(0, 1)
    x_send(1, 3)
    h_send(10)
    y_far(0, 0)
    rotate(1)
    y_own(0, 2)
    partial(0, 0, 0)
    rs_hop(0, 0, 0, 4)
    y_near(0, 1, 0)
    y_near(0, 1, 1)
    partial(0, 1, 0)
    rs_hop(0, 1, 1, 4)
    y_own(0, 3)
    h_send(11)
    y_own(1, 0)
    y_near(0, 2, 0)
    y_near(0, 2, 1)
    y_own(1, 1)
    y_far(0, 1)
    partial(0, 0, 1)
    rs_hop(0, 0, 0, 3)
    rs_hop(0, 0, 1, 3)
    partial(0, 1, 1)
    h_send(12)
    rs_hop(0, 1, 0, 3)
    rs_hop(0, 1, 1, 3)
    y_own(1, 2)
    y_near(0, 3, 0)
    y_near(0, 3, 1)
    y_near(1, 0, 0)
    y_near(1, 0, 1)
    y_own(1, 3)
    y_far(0, 2)
    partial(0, 0, 2)
    rs_hop(0, 0, 0, 2)
    h_send(13)
    rs_hop(0, 0, 1, 2)
    partial(0, 1, 2)
    y_near(1, 1, 0)
    y_near(1, 1, 1)
    rs_hop(0, 1, 0, 2)
    rs_hop(0, 1, 1, 2)
    h_send(14)
    rotate(2)
    y_near(1, 2, 0)
    y_near(1, 2, 1)
    partial(0, 2, 0)
    rs_hop(0, 2, 0, 4)
    partial(0, 2, 1)
    y_far(0, 3)
    h_send(15)
    rs_hop(0, 2, 1, 3)
    y_far(1, 0)
    partial(0, 2, 2)
    partial(0, 0, 3)
    rs_hop(0, 0, 0, 1)
    rs_hop(0, 0, 1, 1)
    partial(0, 1, 3)
    rs_hop(0, 1, 0, 1)
    rs_hop(0, 1, 1, 1)
    rs_hop(0, 2, 0, 3)
    partial(0, 2, 3)
    rs_hop(0, 2, 1, 2)
    y_near(1, 3, 0)
    y_near(1, 3, 1)
    partial(1, 0, 0)
    rs_hop(1, 0, 0, 4)
    partial(1, 1, 0)
    rs_hop(1, 1, 1, 4)
    y_far(1, 1)
    partial(1, 2, 0)
    rs_hop(1, 2, 0, 4)
    rs_final(0, 0)
    y_far(1, 2)
    partial(1, 0, 1)
    rs_hop(1, 0, 1, 3)
    partial(1, 1, 1)
    rs_hop(1, 1, 0, 3)
    partial(1, 0, 2)
    rs_hop(0, 2, 0, 2)
    y_far(1, 3)
    rs_hop(0, 2, 1, 1)
    partial(1, 1, 2)
    partial(1, 2, 1)
    rs_hop(1, 0, 0, 3)
    rs_hop(1, 1, 1, 3)
    rs_hop(1, 2, 1, 3)
    partial(1, 0, 3)
    partial(1, 1, 3)
    rs_hop(1, 0, 1, 2)
    rs_hop(1, 2, 0, 3)
    partial(1, 2, 2)
    partial(1, 2, 3)
    rs_hop(1, 1, 0, 2)
    rotate(3)
    rs_hop(0, 2, 0, 1)
    rs_hop(1, 1, 1, 2)
    partial(0, 3, 0)
    rs_hop(0, 3, 1, 4)
    partial(0, 3, 1)
    rs_hop(1, 0, 0, 2)
    rs_hop(0, 3, 0, 3)
    rs_hop(1, 2, 1, 2)
    partial(0, 3, 2)
    partial(0, 3, 3)
    rs_hop(1, 0, 1, 1)
    rs_hop(1, 2, 0, 2)
    partial(1, 3, 0)
    rs_hop(1, 3, 1, 4)
    partial(1, 3, 1)
    rs_hop(1, 1, 0, 1)
    rs_hop(1, 1, 1, 1)
    rs_hop(1, 3, 0, 3)
    partial(1, 3, 2)
    partial(1, 3, 3)
    rs_hop(0, 3, 1, 3)
    rs_final(0, 1)
    rs_final(0, 2)
    rs_hop(1, 0, 0, 1)
    rs_hop(1, 2, 1, 1)
    rs_hop(0, 3, 0, 2)
    rs_hop(1, 2, 0, 1)
    rs_hop(1, 3, 1, 3)
    rs_final(1, 1)
    rs_hop(1, 3, 0, 2)
    rs_hop(0, 3, 1, 2)
    rs_final(1, 0)
    rs_hop(0, 3, 0, 1)
    rs_hop(1, 3, 1, 2)
    rs_final(1, 2)
    rs_hop(0, 3, 1, 1)
    rs_hop(1, 3, 0, 1)
    rs_hop(1, 3, 1, 1)
    rs_final(0, 3)
    rs_final(1, 3)

    for c in sent:
        c.wait_send()
    for j, g in crossing:
        x_finish(j, g)


def body(gate_pre, up_pre, down_weight):
    hmat = jnp.asarray(np.kron(paley_matrix(), sylvester(32)), BF)
    dma = pltpu.SemaphoreType.DMA
    any_spec = pl.BlockSpec(memory_space=pl.ANY)
    return pl.pallas_call(
        functools.partial(kernel, 1.0 / math.sqrt(16 * KL)),
        out_shape=jax.ShapeDtypeStruct((2 * CW, TOKENS), BF),
        in_specs=[any_spec] * 4,
        out_specs=pl.BlockSpec(memory_space=pltpu.VMEM),
        scratch_shapes=[
            pltpu.VMEM((KL, TOKENS), BF),
            pltpu.VMEM((KL, TOKENS), BF),
            pltpu.VMEM((KL, KL), BF),
            pltpu.VMEM((2, TOKENS, KL), BF),
            pltpu.VMEM((TOKENS, 2 * KL), BF),
            pltpu.VMEM((2, NZ, KB, CW), BF),
            pltpu.VMEM((2, NZ, KB, CW), BF),
            pltpu.VMEM((2, KB, NZ * CW), BF),
            pltpu.VMEM((2, 2 * KL, NZ * CW), BF),
            pltpu.VMEM((2, TOKENS, NZ * CW), F32),
            pltpu.VMEM((2 * NQ, 2, 4, TQ, CW), BF),
            pltpu.VMEM((2 * NQ, 2, 4, TQ, CW), BF),
            dma((5,)),
            dma((2, NZ)), dma((2, NZ)),
            dma((2, NZ)), dma((2, NZ)),
            dma((2, NG, 2)), dma((2, NG, 2)),
            dma((2, NG, 4)), dma((2, NG, 4)),
            dma((2, NG, 4)), dma((2, NG, 4)),
            dma((TOKENS // HX,)), dma((TOKENS // HX,)),
            dma((2 * NQ, 2, 4)), dma((2 * NQ, 2, 4)),
        ],
        compiler_params=pltpu.CompilerParams(
            collective_id=0, has_side_effects=True, vmem_limit_bytes=56 << 20),
        name=NAME,
    )(gate_pre.reshape(KL, TOKENS), up_pre.reshape(KL, TOKENS),
      down_weight.reshape(KL, 16 * 2 * CW), hmat)


def solution(mesh):
    in_specs = (P(None, "tensor", "dp"), P(None, "tensor", "dp"), P(None, "tensor", None))
    out_specs = P("tensor", "dp")
    return jax.shard_map(body, mesh=mesh, in_specs=in_specs, out_specs=out_specs, check_vma=False)
```

```python
import functools
import math

import jax
import jax.numpy as jnp
import numpy as np
from jax import lax
from jax.experimental import pallas as pl
from jax.experimental.pallas import tpu as pltpu
from jax.sharding import PartitionSpec as P

MESH = pl.DeviceIdType.MESH
BF = jnp.bfloat16
F32 = jnp.float32

NZ = 8
KL = 896
KB = 112
TOKENS = 1024
TH = 512
TQ = 256
NQ = TOKENS // TQ
HX = 64
CW = 128


def character(value, prime_order):
    residue = value % prime_order
    if residue == 0:
        return 0
    squares_list = [index * index % prime_order for index in range(1, prime_order)]
    return 1 if residue in squares_list else -1


def paley_matrix():
    prime_order = 13
    conference = np.zeros((14, 14))
    conference[0, 1:] = 1.0
    conference[1:, 0] = 1.0
    for row_index in range(prime_order):
        for col_index in range(prime_order):
            conference[row_index + 1, col_index + 1] = character(col_index - row_index, prime_order)
    first = np.array([[1.0, 1.0], [1.0, -1.0]])
    second = np.array([[1.0, -1.0], [-1.0, -1.0]])
    return np.kron(conference, first) + np.kron(np.eye(14), second)


def sylvester(order):
    matrix = np.ones((1, 1))
    basic = np.array([[1.0, 1.0], [1.0, -1.0]])
    while matrix.shape[0] < order:
        matrix = np.kron(basic, matrix)
    return matrix


def place(d):
    d %= NZ
    return max(0, 2 * (4 - d) - 1) if d <= 4 else 2 * (d - 4)


GROUPS = ((0, 1), (1, 2), (3, 2), (5, 3))
NG = len(GROUPS)


def chain(q, k):
    return (1, 4 - q % 2) if k == 0 else (-1, 3 + q % 2)


NAME = "rotated_down_projection"


def kernel(scale, gate, up, weight, hmat, out,
           gbuf, ubuf, hbuf, hid, rot, rec1, snd2, stg, wbuf, part, rsend, rrecv,
           load_sem, p1s, p1r, p2s, p2r, xs, xr, ys, yr, cs, cr, hs, hr, rs, rr):
    dp = lax.axis_index("dp")
    tn = lax.axis_index("tensor")
    y = dp // 4
    xl = lax.rem(dp // 2, 2)
    core = lax.rem(dp, 2)
    xh = tn // NZ
    z = lax.rem(tn, NZ)
    block = y * 2 + xl
    crossed = core != xh

    def dev(y_=None, xl_=None, core_=None, xh_=None, z_=None):
        y_ = y if y_ is None else y_
        xl_ = xl if xl_ is None else xl_
        core_ = core if core_ is None else core_
        xh_ = xh if xh_ is None else xh_
        z_ = z if z_ is None else z_
        return (y_ * 4 + xl_ * 2 + core_, xh_ * NZ + z_)

    def zat(o):
        return lax.rem(z + (o % NZ), NZ)

    def yat(o):
        return lax.rem(y + (o % 4), 4)

    def remote(src, dst, s, r, to):
        return pltpu.make_async_remote_copy(
            src_ref=src, dst_ref=dst, send_sem=s, recv_sem=r, device_id=to, device_id_type=MESH)

    sent = []

    def send(src, dst, s, r, to):
        c = remote(src, dst, s, r, to)
        c.start()
        sent.append(c)

    def recv(dst, s, r, frm):
        remote(dst, dst, s, r, frm).wait_recv()

    loads = []

    def load(src, dst):
        c = pltpu.make_async_copy(src, dst, load_sem.at[len(loads)])
        c.start()
        loads.append(c)

    def load_all():
        for t in range(2):
            ts = pl.ds(t * TH, TH)
            load(gate.at[:, ts], gbuf.at[:, ts])
            load(up.at[:, ts], ubuf.at[:, ts])
        load(hmat, hbuf)

    barrier = pltpu.get_barrier_semaphore()
    partners = [dev(z_=zat(o)) for o in range(1, NZ)]
    partners += [dev(y_=yat(1)), dev(y_=yat(-1)), dev(core_=1 - core), dev(xh_=1 - xh)]
    partners += [dev(xl_=1 - xl, core_=xh, xh_=core)]
    for to in partners:
        pl.semaphore_signal(barrier, inc=1, device_id=to, device_id_type=MESH)

    @pl.when(crossed)
    def _():
        pl.semaphore_signal(barrier, inc=1, device_id=dev(core_=xh, xh_=core), device_id_type=MESH)

    def meet():
        @pl.when(crossed)
        def _():
            pl.semaphore_wait(barrier, len(partners) + 1)

        @pl.when(jnp.logical_not(crossed))
        def _():
            pl.semaphore_wait(barrier, len(partners))

    rows1 = pl.ds(pl.multiple_of(block * KB, 16), KB)

    def cols1(j, zz):
        return pl.ds(pl.multiple_of(core * (NZ * 2 * CW) + zz * (2 * CW) + j * CW, 128), CW)

    def p1_send(j):
        for o in range(1, NZ):
            zz = zat(o)
            send(weight.at[rows1, cols1(j, zz)], rec1.at[j, z], p1s.at[j, o], p1r.at[j, o], dev(z_=zz))
        pltpu.make_async_copy(weight.at[rows1, cols1(j, z)], rec1.at[j, z], p1r.at[j, 0]).start()

    def p1_wait_rotate(j):
        pltpu.make_async_copy(weight.at[rows1, cols1(j, z)], rec1.at[j, z], p1r.at[j, 0]).wait()
        for o in range(1, NZ):
            zz = zat(-o)
            recv(rec1.at[j, zz], p1s.at[j, o], p1r.at[j, o], dev(z_=zz))
        v = [rec1[j, i].astype(F32) for i in range(NZ)]
        for bit in (1, 2, 4):
            v = [v[i] + v[i ^ bit] if not i & bit else v[i ^ bit] - v[i] for i in range(NZ)]
        for i in range(NZ):
            snd2[j, i] = v[i].astype(BF)

    def p2_send(j):
        for o in sorted(range(1, NZ), key=lambda o: place(-o)):
            zz = zat(o)
            send(snd2.at[j, zz], stg.at[j, :, pl.ds(place(-o) * CW, CW)], p2s.at[j, o], p2r.at[j, o], dev(z_=zz))
        stg[j, :, pl.ds(place(0) * CW, CW)] = snd2[j, z]

    def gcols(g):
        return pl.ds(GROUPS[g][0] * CW, GROUPS[g][1] * CW)

    def wrows(s, b, n):
        return pl.ds(pl.multiple_of(s * KL + b * KB, 16), n)

    def x_copy(j, g, dst_xl, i):
        return remote(stg.at[j, :, gcols(g)], wbuf.at[j, wrows(xh, block, KB), gcols(g)],
                      xs.at[j, g, i], xr.at[j, g, i], dev(xl_=dst_xl, core_=xh, xh_=core))

    crossing = []

    def x_send(j, g):
        crossing.append((j, g))
        for o in range(1, NZ):
            if 0 <= place(-o) - GROUPS[g][0] < GROUPS[g][1]:
                recv(stg.at[j, :, pl.ds(place(-o) * CW, CW)], p2s.at[j, o], p2r.at[j, o], dev(z_=zat(-o)))
        c = x_copy(j, g, 1 - xl, 1)
        c.start()
        sent.append(c)

        @pl.when(crossed)
        def _():
            x_copy(j, g, xl, 0).start()

        @pl.when(jnp.logical_not(crossed))
        def _():
            pltpu.make_async_copy(stg.at[j, :, gcols(g)], wbuf.at[j, wrows(xh, block, KB), gcols(g)],
                                  xr.at[j, g, 0]).start()

    def x_finish(j, g):
        @pl.when(crossed)
        def _():
            x_copy(j, g, xl, 0).wait_send()

    def wblock(j, g, s, yy, n=2 * KB, off=0):
        return wbuf.at[j, wrows(s, yy * 2 + off, n), gcols(g)]

    def core_fwd(j, g, yy, i):
        ref = wblock(j, g, core, yy)
        send(ref, ref, cs.at[j, g, i], cr.at[j, g, i], dev(core_=1 - core))

    def y_own(j, g):
        own = wbuf.at[j, wrows(core, block, KB), gcols(g)]
        recv(own, xs.at[j, g, 0], xr.at[j, g, 0], dev(core_=xh, xh_=core))
        other = wbuf.at[j, wrows(core, y * 2 + 1 - xl, KB), gcols(g)]
        recv(other, xs.at[j, g, 1], xr.at[j, g, 1], dev(xl_=1 - xl, core_=xh, xh_=core))
        ref = wblock(j, g, core, y)
        send(ref, ref, ys.at[j, g, 0], yr.at[j, g, 0], dev(y_=yat(1)))
        send(ref, ref, ys.at[j, g, 1], yr.at[j, g, 1], dev(y_=yat(-1)))
        core_fwd(j, g, y, 0)

    def y_near(j, g, i):
        step = 1 - 2 * i
        frm = yat(-step)
        recv(wblock(j, g, core, frm), ys.at[j, g, i], yr.at[j, g, i], dev(y_=frm))
        half = wblock(j, g, core, frm, KB, i)
        send(half, half, ys.at[j, g, 2 + i], yr.at[j, g, 2 + i], dev(y_=yat(step)))
        core_fwd(j, g, frm, 1 + i)

    def y_far(j, g):
        far = yat(2)
        for i, step in ((0, 1), (1, -1)):
            recv(wblock(j, g, core, far, KB, i), ys.at[j, g, 2 + i], yr.at[j, g, 2 + i], dev(y_=yat(-step)))
        core_fwd(j, g, far, 3)

    def w_wait(j, g):
        for i, o in enumerate((0, -1, 1, 2)):
            recv(wblock(j, g, 1 - core, yat(o)), cs.at[j, g, i], cr.at[j, g, i], dev(core_=1 - core))

    def silu(t):
        loads[2 * t].wait()
        loads[2 * t + 1].wait()

        def step(i, carry):
            rows = pl.ds(pl.multiple_of(i * 128, 128), 128)
            cols = pl.ds(t * TH, TH)
            half = gbuf[rows, cols].astype(F32) * 0.5
            value = (half + half * jnp.tanh(half)) * ubuf[rows, cols].astype(F32)
            hid[xh, cols, rows] = value.astype(BF).T
            return carry

        lax.fori_loop(0, KL // 128, step, 0)

    def h_ref(q, s):
        return hid.at[s, pl.ds(q * HX, HX)]

    def h_send(q):
        send(h_ref(q, xh), h_ref(q, xh), hs.at[q], hr.at[q], dev(xh_=1 - xh))

    def rotate(q):
        if not rotated:
            loads[4].wait()
        rotated.add(q)
        for i in range(q * TQ // HX, (q + 1) * TQ // HX):
            recv(h_ref(i, 1 - xh), hs.at[i], hr.at[i], dev(xh_=1 - xh))
        rows = pl.ds(q * TQ, TQ)
        for n0, n in ((0, 256), (256, 256), (512, 256), (768, 128)):
            m = hbuf[:, n0:n0 + n]
            l0 = jnp.dot(hid[0, rows], m, preferred_element_type=F32)
            l1 = jnp.dot(hid[1, rows], m, preferred_element_type=F32)
            rot[rows, n0:n0 + n] = ((l0 + l1) * scale).astype(BF)
            rot[rows, KL + n0:KL + n0 + n] = ((l0 - l1) * scale).astype(BF)

    rotated = set()
    complete = set()

    def partial(j, q, g):
        if (j, g) not in complete:
            w_wait(j, g)
            complete.add((j, g))
        first, n = GROUPS[g]
        for i in range(0, n, 2):
            w = min(2, n - i) * CW
            c0 = (first + i) * CW
            part[j, pl.ds(q * TQ, TQ), c0:c0 + w] = jnp.dot(
                rot[pl.ds(q * TQ, TQ)], wbuf[j, :, c0:c0 + w], preferred_element_type=F32)

    def own_part(j, q, m):
        c0 = place(m) * CW
        return part[j, pl.ds(q * TQ, TQ), c0:c0 + CW]

    def rs_wait(j, q, k, m):
        p = j * NQ + q
        recv(rrecv.at[p, k, m], rs.at[p, k, m], rr.at[p, k, m], dev(z_=zat(-chain(q, k)[0])))
        return rrecv[p, k, m].astype(F32)

    def rs_hop(j, q, k, m):
        p = j * NQ + q
        d, first = chain(q, k)
        value = own_part(j, q, d * m)
        if m < first:
            value = value + rs_wait(j, q, k, m)
        rsend[p, k, m - 1] = value.astype(BF)
        send(rsend.at[p, k, m - 1], rrecv.at[p, k, m - 1], rs.at[p, k, m - 1], rr.at[p, k, m - 1],
             dev(z_=zat(d)))

    def rs_final(j, q):
        value = own_part(j, q, 0) + rs_wait(j, q, 0, 0) + rs_wait(j, q, 1, 0)
        out[j * CW:(j + 1) * CW, q * TQ:(q + 1) * TQ] = value.T.astype(BF)

    load_all()
    silu(0)
    meet()
    p1_send(0)
    p1_send(1)
    h_send(0)
    h_send(1)
    h_send(2)
    silu(1)
    h_send(3)
    p1_wait_rotate(0)
    p2_send(0)
    h_send(4)
    h_send(5)
    p1_wait_rotate(1)
    p2_send(1)
    x_send(0, 0)
    h_send(6)
    rotate(0)
    x_send(0, 1)
    h_send(7)
    x_send(0, 2)
    x_send(0, 3)
    h_send(8)
    x_send(1, 0)
    y_own(0, 0)
    x_send(1, 1)
    h_send(9)
    x_send(1, 2)
    y_near(0, 0, 0)
    y_near(0, 0, 1)
    y_own(0, 1)
    x_send(1, 3)
    h_send(10)
    y_far(0, 0)
    rotate(1)
    y_own(0, 2)
    partial(0, 0, 0)
    rs_hop(0, 0, 0, 4)
    y_near(0, 1, 0)
    y_near(0, 1, 1)
    partial(0, 1, 0)
    rs_hop(0, 1, 1, 4)
    y_own(0, 3)
    h_send(11)
    y_own(1, 0)
    y_near(0, 2, 0)
    y_near(0, 2, 1)
    y_own(1, 1)
    y_far(0, 1)
    partial(0, 0, 1)
    rs_hop(0, 0, 0, 3)
    rs_hop(0, 0, 1, 3)
    partial(0, 1, 1)
    h_send(12)
    rs_hop(0, 1, 0, 3)
    rs_hop(0, 1, 1, 3)
    y_own(1, 2)
    y_near(0, 3, 0)
    y_near(0, 3, 1)
    y_near(1, 0, 0)
    y_near(1, 0, 1)
    y_own(1, 3)
    y_far(0, 2)
    partial(0, 0, 2)
    rs_hop(0, 0, 0, 2)
    h_send(13)
    rs_hop(0, 0, 1, 2)
    partial(0, 1, 2)
    y_near(1, 1, 0)
    y_near(1, 1, 1)
    rs_hop(0, 1, 0, 2)
    rs_hop(0, 1, 1, 2)
    h_send(14)
    rotate(2)
    y_near(1, 2, 0)
    y_near(1, 2, 1)
    partial(0, 2, 0)
    rs_hop(0, 2, 0, 4)
    partial(0, 2, 1)
    y_far(0, 3)
    h_send(15)
    rs_hop(0, 2, 1, 3)
    y_far(1, 0)
    partial(0, 2, 2)
    partial(0, 0, 3)
    rs_hop(0, 0, 0, 1)
    rs_hop(0, 0, 1, 1)
    partial(0, 1, 3)
    rs_hop(0, 1, 0, 1)
    rs_hop(0, 1, 1, 1)
    rs_hop(0, 2, 0, 3)
    partial(0, 2, 3)
    rs_hop(0, 2, 1, 2)
    y_near(1, 3, 0)
    y_near(1, 3, 1)
    partial(1, 0, 0)
    rs_hop(1, 0, 0, 4)
    partial(1, 1, 0)
    rs_hop(1, 1, 1, 4)
    y_far(1, 1)
    partial(1, 2, 0)
    rs_hop(1, 2, 0, 4)
    rs_final(0, 0)
    y_far(1, 2)
    partial(1, 0, 1)
    rs_hop(1, 0, 1, 3)
    partial(1, 1, 1)
    rs_hop(1, 1, 0, 3)
    partial(1, 0, 2)
    rs_hop(0, 2, 0, 2)
    y_far(1, 3)
    rs_hop(0, 2, 1, 1)
    partial(1, 1, 2)
    partial(1, 2, 1)
    rs_hop(1, 0, 0, 3)
    rs_hop(1, 1, 1, 3)
    rs_hop(1, 2, 1, 3)
    partial(1, 0, 3)
    partial(1, 1, 3)
    rs_hop(1, 0, 1, 2)
    rs_hop(1, 2, 0, 3)
    partial(1, 2, 2)
    partial(1, 2, 3)
    rs_hop(1, 1, 0, 2)
    rotate(3)
    rs_hop(0, 2, 0, 1)
    rs_hop(1, 1, 1, 2)
    partial(0, 3, 0)
    rs_hop(0, 3, 1, 4)
    partial(0, 3, 1)
    rs_hop(1, 0, 0, 2)
    rs_hop(0, 3, 0, 3)
    rs_hop(1, 2, 1, 2)
    partial(0, 3, 2)
    partial(0, 3, 3)
    rs_hop(1, 0, 1, 1)
    rs_hop(1, 2, 0, 2)
    partial(1, 3, 0)
    rs_hop(1, 3, 1, 4)
    partial(1, 3, 1)
    rs_hop(1, 1, 0, 1)
    rs_hop(1, 1, 1, 1)
    rs_hop(1, 3, 0, 3)
    partial(1, 3, 2)
    partial(1, 3, 3)
    rs_hop(0, 3, 1, 3)
    rs_final(0, 1)
    rs_final(0, 2)
    rs_hop(1, 0, 0, 1)
    rs_hop(1, 2, 1, 1)
    rs_hop(0, 3, 0, 2)
    rs_hop(1, 2, 0, 1)
    rs_hop(1, 3, 1, 3)
    rs_final(1, 1)
    rs_hop(1, 3, 0, 2)
    rs_hop(0, 3, 1, 2)
    rs_final(1, 0)
    rs_hop(0, 3, 0, 1)
    rs_hop(1, 3, 1, 2)
    rs_final(1, 2)
    rs_hop(0, 3, 1, 1)
    rs_hop(1, 3, 0, 1)
    rs_hop(1, 3, 1, 1)
    rs_final(0, 3)
    rs_final(1, 3)

    for c in sent:
        c.wait_send()
    for j, g in crossing:
        x_finish(j, g)


def body(gate_pre, up_pre, down_weight):
    hmat = jnp.asarray(np.kron(paley_matrix(), sylvester(32)), BF)
    dma = pltpu.SemaphoreType.DMA
    any_spec = pl.BlockSpec(memory_space=pl.ANY)
    return pl.pallas_call(
        functools.partial(kernel, 1.0 / math.sqrt(16 * KL)),
        out_shape=jax.ShapeDtypeStruct((2 * CW, TOKENS), BF),
        in_specs=[any_spec] * 4,
        out_specs=pl.BlockSpec(memory_space=pltpu.VMEM),
        scratch_shapes=[
            pltpu.VMEM((KL, TOKENS), BF),
            pltpu.VMEM((KL, TOKENS), BF),
            pltpu.VMEM((KL, KL), BF),
            pltpu.VMEM((2, TOKENS, KL), BF),
            pltpu.VMEM((TOKENS, 2 * KL), BF),
            pltpu.VMEM((2, NZ, KB, CW), BF),
            pltpu.VMEM((2, NZ, KB, CW), BF),
            pltpu.VMEM((2, KB, NZ * CW), BF),
            pltpu.VMEM((2, 2 * KL, NZ * CW), BF),
            pltpu.VMEM((2, TOKENS, NZ * CW), F32),
            pltpu.VMEM((2 * NQ, 2, 4, TQ, CW), BF),
            pltpu.VMEM((2 * NQ, 2, 4, TQ, CW), BF),
            dma((5,)),
            dma((2, NZ)), dma((2, NZ)),
            dma((2, NZ)), dma((2, NZ)),
            dma((2, NG, 2)), dma((2, NG, 2)),
            dma((2, NG, 4)), dma((2, NG, 4)),
            dma((2, NG, 4)), dma((2, NG, 4)),
            dma((TOKENS // HX,)), dma((TOKENS // HX,)),
            dma((2 * NQ, 2, 4)), dma((2 * NQ, 2, 4)),
        ],
        compiler_params=pltpu.CompilerParams(
            collective_id=0, has_side_effects=True, vmem_limit_bytes=56 << 20),
        name=NAME,
    )(gate_pre.reshape(KL, TOKENS), up_pre.reshape(KL, TOKENS),
      down_weight.reshape(KL, 16 * 2 * CW), hmat)


def solution(mesh):
    in_specs = (P(None, "tensor", "dp"), P(None, "tensor", "dp"), P(None, "tensor", None))
    out_specs = P("tensor", "dp")
    return jax.shard_map(body, mesh=mesh, in_specs=in_specs, out_specs=out_specs, check_vma=False)
```

```python
import functools
import math

import jax
import jax.numpy as jnp
import numpy as np
from jax import lax
from jax.experimental import pallas as pl
from jax.experimental.pallas import tpu as pltpu
from jax.sharding import PartitionSpec as P

MESH = pl.DeviceIdType.MESH
BF = jnp.bfloat16
F32 = jnp.float32

NZ = 8
KL = 896
KB = 112
TOKENS = 1024
TH = 512
TQ = 256
NQ = TOKENS // TQ
HX = 64
CW = 128


def character(value, prime_order):
    residue = value % prime_order
    if residue == 0:
        return 0
    squares_list = [index * index % prime_order for index in range(1, prime_order)]
    return 1 if residue in squares_list else -1


def paley_matrix():
    prime_order = 13
    conference = np.zeros((14, 14))
    conference[0, 1:] = 1.0
    conference[1:, 0] = 1.0
    for row_index in range(prime_order):
        for col_index in range(prime_order):
            conference[row_index + 1, col_index + 1] = character(col_index - row_index, prime_order)
    first = np.array([[1.0, 1.0], [1.0, -1.0]])
    second = np.array([[1.0, -1.0], [-1.0, -1.0]])
    return np.kron(conference, first) + np.kron(np.eye(14), second)


def sylvester(order):
    matrix = np.ones((1, 1))
    basic = np.array([[1.0, 1.0], [1.0, -1.0]])
    while matrix.shape[0] < order:
        matrix = np.kron(basic, matrix)
    return matrix


def place(d):
    d %= NZ
    return max(0, 2 * (4 - d) - 1) if d <= 4 else 2 * (d - 4)


GROUPS = ((0, 1), (1, 2), (3, 2), (5, 3))
NG = len(GROUPS)


def chain(q, k):
    return (1, 4 - q % 2) if k == 0 else (-1, 3 + q % 2)


NAME = "rotated_down_projection"


def kernel(scale, gate, up, weight, hmat, out,
           gbuf, ubuf, hbuf, hid, rot, rec1, snd2, stg, wbuf, part, rsend, rrecv,
           load_sem, p1s, p1r, p2s, p2r, xs, xr, ys, yr, cs, cr, hs, hr, rs, rr):
    dp = lax.axis_index("dp")
    tn = lax.axis_index("tensor")
    y = dp // 4
    xl = lax.rem(dp // 2, 2)
    core = lax.rem(dp, 2)
    xh = tn // NZ
    z = lax.rem(tn, NZ)
    block = y * 2 + xl
    crossed = core != xh

    def dev(y_=None, xl_=None, core_=None, xh_=None, z_=None):
        y_ = y if y_ is None else y_
        xl_ = xl if xl_ is None else xl_
        core_ = core if core_ is None else core_
        xh_ = xh if xh_ is None else xh_
        z_ = z if z_ is None else z_
        return (y_ * 4 + xl_ * 2 + core_, xh_ * NZ + z_)

    def zat(o):
        return lax.rem(z + (o % NZ), NZ)

    def yat(o):
        return lax.rem(y + (o % 4), 4)

    def remote(src, dst, s, r, to):
        return pltpu.make_async_remote_copy(
            src_ref=src, dst_ref=dst, send_sem=s, recv_sem=r, device_id=to, device_id_type=MESH)

    sent = []

    def send(src, dst, s, r, to):
        c = remote(src, dst, s, r, to)
        c.start()
        sent.append(c)

    def recv(dst, s, r, frm):
        remote(dst, dst, s, r, frm).wait_recv()

    loads = []

    def load(src, dst):
        c = pltpu.make_async_copy(src, dst, load_sem.at[len(loads)])
        c.start()
        loads.append(c)

    def load_all():
        for t in range(2):
            ts = pl.ds(t * TH, TH)
            load(gate.at[:, ts], gbuf.at[:, ts])
            load(up.at[:, ts], ubuf.at[:, ts])
        load(hmat, hbuf)

    barrier = pltpu.get_barrier_semaphore()
    partners = [dev(z_=zat(o)) for o in range(1, NZ)]
    partners += [dev(y_=yat(1)), dev(y_=yat(-1)), dev(core_=1 - core), dev(xh_=1 - xh)]
    partners += [dev(xl_=1 - xl, core_=xh, xh_=core)]
    for to in partners:
        pl.semaphore_signal(barrier, inc=1, device_id=to, device_id_type=MESH)

    @pl.when(crossed)
    def _():
        pl.semaphore_signal(barrier, inc=1, device_id=dev(core_=xh, xh_=core), device_id_type=MESH)

    def meet():
        @pl.when(crossed)
        def _():
            pl.semaphore_wait(barrier, len(partners) + 1)

        @pl.when(jnp.logical_not(crossed))
        def _():
            pl.semaphore_wait(barrier, len(partners))

    rows1 = pl.ds(pl.multiple_of(block * KB, 16), KB)

    def cols1(j, zz):
        return pl.ds(pl.multiple_of(core * (NZ * 2 * CW) + zz * (2 * CW) + j * CW, 128), CW)

    def p1_send(j):
        for o in range(1, NZ):
            zz = zat(o)
            send(weight.at[rows1, cols1(j, zz)], rec1.at[j, z], p1s.at[j, o], p1r.at[j, o], dev(z_=zz))
        pltpu.make_async_copy(weight.at[rows1, cols1(j, z)], rec1.at[j, z], p1r.at[j, 0]).start()

    def p1_wait_rotate(j):
        pltpu.make_async_copy(weight.at[rows1, cols1(j, z)], rec1.at[j, z], p1r.at[j, 0]).wait()
        for o in range(1, NZ):
            zz = zat(-o)
            recv(rec1.at[j, zz], p1s.at[j, o], p1r.at[j, o], dev(z_=zz))
        v = [rec1[j, i].astype(F32) for i in range(NZ)]
        for bit in (1, 2, 4):
            v = [v[i] + v[i ^ bit] if not i & bit else v[i ^ bit] - v[i] for i in range(NZ)]
        for i in range(NZ):
            snd2[j, i] = v[i].astype(BF)

    def p2_send(j):
        for o in sorted(range(1, NZ), key=lambda o: place(-o)):
            zz = zat(o)
            send(snd2.at[j, zz], stg.at[j, :, pl.ds(place(-o) * CW, CW)], p2s.at[j, o], p2r.at[j, o], dev(z_=zz))
        stg[j, :, pl.ds(place(0) * CW, CW)] = snd2[j, z]

    def gcols(g):
        return pl.ds(GROUPS[g][0] * CW, GROUPS[g][1] * CW)

    def wrows(s, b, n):
        return pl.ds(pl.multiple_of(s * KL + b * KB, 16), n)

    def x_copy(j, g, dst_xl, i):
        return remote(stg.at[j, :, gcols(g)], wbuf.at[j, wrows(xh, block, KB), gcols(g)],
                      xs.at[j, g, i], xr.at[j, g, i], dev(xl_=dst_xl, core_=xh, xh_=core))

    crossing = []

    def x_send(j, g):
        crossing.append((j, g))
        for o in range(1, NZ):
            if 0 <= place(-o) - GROUPS[g][0] < GROUPS[g][1]:
                recv(stg.at[j, :, pl.ds(place(-o) * CW, CW)], p2s.at[j, o], p2r.at[j, o], dev(z_=zat(-o)))
        c = x_copy(j, g, 1 - xl, 1)
        c.start()
        sent.append(c)

        @pl.when(crossed)
        def _():
            x_copy(j, g, xl, 0).start()

        @pl.when(jnp.logical_not(crossed))
        def _():
            pltpu.make_async_copy(stg.at[j, :, gcols(g)], wbuf.at[j, wrows(xh, block, KB), gcols(g)],
                                  xr.at[j, g, 0]).start()

    def x_finish(j, g):
        @pl.when(crossed)
        def _():
            x_copy(j, g, xl, 0).wait_send()

    def wblock(j, g, s, yy, n=2 * KB, off=0):
        return wbuf.at[j, wrows(s, yy * 2 + off, n), gcols(g)]

    def core_fwd(j, g, yy, i):
        ref = wblock(j, g, core, yy)
        send(ref, ref, cs.at[j, g, i], cr.at[j, g, i], dev(core_=1 - core))

    def y_own(j, g):
        own = wbuf.at[j, wrows(core, block, KB), gcols(g)]
        recv(own, xs.at[j, g, 0], xr.at[j, g, 0], dev(core_=xh, xh_=core))
        other = wbuf.at[j, wrows(core, y * 2 + 1 - xl, KB), gcols(g)]
        recv(other, xs.at[j, g, 1], xr.at[j, g, 1], dev(xl_=1 - xl, core_=xh, xh_=core))
        ref = wblock(j, g, core, y)
        send(ref, ref, ys.at[j, g, 0], yr.at[j, g, 0], dev(y_=yat(1)))
        send(ref, ref, ys.at[j, g, 1], yr.at[j, g, 1], dev(y_=yat(-1)))
        core_fwd(j, g, y, 0)

    def y_near(j, g, i):
        step = 1 - 2 * i
        frm = yat(-step)
        recv(wblock(j, g, core, frm), ys.at[j, g, i], yr.at[j, g, i], dev(y_=frm))
        half = wblock(j, g, core, frm, KB, i)
        send(half, half, ys.at[j, g, 2 + i], yr.at[j, g, 2 + i], dev(y_=yat(step)))
        core_fwd(j, g, frm, 1 + i)

    def y_far(j, g):
        far = yat(2)
        for i, step in ((0, 1), (1, -1)):
            recv(wblock(j, g, core, far, KB, i), ys.at[j, g, 2 + i], yr.at[j, g, 2 + i], dev(y_=yat(-step)))
        core_fwd(j, g, far, 3)

    def w_wait(j, g):
        for i, o in enumerate((0, -1, 1, 2)):
            recv(wblock(j, g, 1 - core, yat(o)), cs.at[j, g, i], cr.at[j, g, i], dev(core_=1 - core))

    def silu(t):
        loads[2 * t].wait()
        loads[2 * t + 1].wait()

        def step(i, carry):
            rows = pl.ds(pl.multiple_of(i * 128, 128), 128)
            cols = pl.ds(t * TH, TH)
            half = gbuf[rows, cols].astype(F32) * 0.5
            value = (half + half * jnp.tanh(half)) * ubuf[rows, cols].astype(F32)
            hid[xh, cols, rows] = value.astype(BF).T
            return carry

        lax.fori_loop(0, KL // 128, step, 0)

    def h_ref(q, s):
        return hid.at[s, pl.ds(q * HX, HX)]

    def h_send(q):
        send(h_ref(q, xh), h_ref(q, xh), hs.at[q], hr.at[q], dev(xh_=1 - xh))

    def rotate(q):
        if not rotated:
            loads[4].wait()
        rotated.add(q)
        for i in range(q * TQ // HX, (q + 1) * TQ // HX):
            recv(h_ref(i, 1 - xh), hs.at[i], hr.at[i], dev(xh_=1 - xh))
        rows = pl.ds(q * TQ, TQ)
        for n0, n in ((0, 256), (256, 256), (512, 256), (768, 128)):
            m = hbuf[:, n0:n0 + n]
            l0 = jnp.dot(hid[0, rows], m, preferred_element_type=F32)
            l1 = jnp.dot(hid[1, rows], m, preferred_element_type=F32)
            rot[rows, n0:n0 + n] = ((l0 + l1) * scale).astype(BF)
            rot[rows, KL + n0:KL + n0 + n] = ((l0 - l1) * scale).astype(BF)

    rotated = set()
    complete = set()

    def partial(j, q, g):
        if (j, g) not in complete:
            w_wait(j, g)
            complete.add((j, g))
        first, n = GROUPS[g]
        for i in range(0, n, 2):
            w = min(2, n - i) * CW
            c0 = (first + i) * CW
            part[j, pl.ds(q * TQ, TQ), c0:c0 + w] = jnp.dot(
                rot[pl.ds(q * TQ, TQ)], wbuf[j, :, c0:c0 + w], preferred_element_type=F32)

    def own_part(j, q, m):
        c0 = place(m) * CW
        return part[j, pl.ds(q * TQ, TQ), c0:c0 + CW]

    def rs_wait(j, q, k, m):
        p = j * NQ + q
        recv(rrecv.at[p, k, m], rs.at[p, k, m], rr.at[p, k, m], dev(z_=zat(-chain(q, k)[0])))
        return rrecv[p, k, m].astype(F32)

    def rs_hop(j, q, k, m):
        p = j * NQ + q
        d, first = chain(q, k)
        value = own_part(j, q, d * m)
        if m < first:
            value = value + rs_wait(j, q, k, m)
        rsend[p, k, m - 1] = value.astype(BF)
        send(rsend.at[p, k, m - 1], rrecv.at[p, k, m - 1], rs.at[p, k, m - 1], rr.at[p, k, m - 1],
             dev(z_=zat(d)))

    def rs_final(j, q):
        value = own_part(j, q, 0) + rs_wait(j, q, 0, 0) + rs_wait(j, q, 1, 0)
        out[q * TQ:(q + 1) * TQ, j * CW:(j + 1) * CW] = value.astype(BF)

    load_all()
    silu(0)
    meet()
    p1_send(0)
    p1_send(1)
    h_send(0)
    h_send(1)
    h_send(2)
    silu(1)
    h_send(3)
    p1_wait_rotate(0)
    p2_send(0)
    h_send(4)
    h_send(5)
    p1_wait_rotate(1)
    p2_send(1)
    x_send(0, 0)
    h_send(6)
    rotate(0)
    x_send(0, 1)
    h_send(7)
    x_send(0, 2)
    x_send(0, 3)
    h_send(8)
    x_send(1, 0)
    y_own(0, 0)
    x_send(1, 1)
    h_send(9)
    x_send(1, 2)
    y_near(0, 0, 0)
    y_near(0, 0, 1)
    y_own(0, 1)
    x_send(1, 3)
    h_send(10)
    y_far(0, 0)
    rotate(1)
    y_own(0, 2)
    partial(0, 0, 0)
    rs_hop(0, 0, 0, 4)
    y_near(0, 1, 0)
    y_near(0, 1, 1)
    partial(0, 1, 0)
    rs_hop(0, 1, 1, 4)
    y_own(0, 3)
    h_send(11)
    y_own(1, 0)
    y_near(0, 2, 0)
    y_near(0, 2, 1)
    y_own(1, 1)
    y_far(0, 1)
    partial(0, 0, 1)
    rs_hop(0, 0, 0, 3)
    rs_hop(0, 0, 1, 3)
    partial(0, 1, 1)
    h_send(12)
    rs_hop(0, 1, 0, 3)
    rs_hop(0, 1, 1, 3)
    y_own(1, 2)
    y_near(0, 3, 0)
    y_near(0, 3, 1)
    y_near(1, 0, 0)
    y_near(1, 0, 1)
    y_own(1, 3)
    y_far(0, 2)
    partial(0, 0, 2)
    rs_hop(0, 0, 0, 2)
    h_send(13)
    rs_hop(0, 0, 1, 2)
    partial(0, 1, 2)
    y_near(1, 1, 0)
    y_near(1, 1, 1)
    rs_hop(0, 1, 0, 2)
    rs_hop(0, 1, 1, 2)
    h_send(14)
    rotate(2)
    y_near(1, 2, 0)
    y_near(1, 2, 1)
    partial(0, 2, 0)
    rs_hop(0, 2, 0, 4)
    partial(0, 2, 1)
    y_far(0, 3)
    h_send(15)
    rs_hop(0, 2, 1, 3)
    y_far(1, 0)
    partial(0, 2, 2)
    partial(0, 0, 3)
    rs_hop(0, 0, 0, 1)
    rs_hop(0, 0, 1, 1)
    partial(0, 1, 3)
    rs_hop(0, 1, 0, 1)
    rs_hop(0, 1, 1, 1)
    rs_hop(0, 2, 0, 3)
    partial(0, 2, 3)
    rs_hop(0, 2, 1, 2)
    y_near(1, 3, 0)
    y_near(1, 3, 1)
    partial(1, 0, 0)
    rs_hop(1, 0, 0, 4)
    partial(1, 1, 0)
    rs_hop(1, 1, 1, 4)
    y_far(1, 1)
    partial(1, 2, 0)
    rs_hop(1, 2, 0, 4)
    rs_final(0, 0)
    y_far(1, 2)
    partial(1, 0, 1)
    rs_hop(1, 0, 1, 3)
    partial(1, 1, 1)
    rs_hop(1, 1, 0, 3)
    partial(1, 0, 2)
    rs_hop(0, 2, 0, 2)
    y_far(1, 3)
    rs_hop(0, 2, 1, 1)
    partial(1, 1, 2)
    partial(1, 2, 1)
    rs_hop(1, 0, 0, 3)
    rs_hop(1, 1, 1, 3)
    rs_hop(1, 2, 1, 3)
    partial(1, 0, 3)
    partial(1, 1, 3)
    rs_hop(1, 0, 1, 2)
    rs_hop(1, 2, 0, 3)
    partial(1, 2, 2)
    partial(1, 2, 3)
    rs_hop(1, 1, 0, 2)
    rotate(3)
    rs_hop(0, 2, 0, 1)
    rs_hop(1, 1, 1, 2)
    partial(0, 3, 0)
    rs_hop(0, 3, 1, 4)
    partial(0, 3, 1)
    rs_hop(1, 0, 0, 2)
    rs_hop(0, 3, 0, 3)
    rs_hop(1, 2, 1, 2)
    partial(0, 3, 2)
    partial(0, 3, 3)
    rs_hop(1, 0, 1, 1)
    rs_hop(1, 2, 0, 2)
    partial(1, 3, 0)
    rs_hop(1, 3, 1, 4)
    partial(1, 3, 1)
    rs_hop(1, 1, 0, 1)
    rs_hop(1, 1, 1, 1)
    rs_hop(1, 3, 0, 3)
    partial(1, 3, 2)
    partial(1, 3, 3)
    rs_hop(0, 3, 1, 3)
    rs_final(0, 1)
    rs_final(0, 2)
    rs_hop(1, 0, 0, 1)
    rs_hop(1, 2, 1, 1)
    rs_hop(0, 3, 0, 2)
    rs_hop(1, 2, 0, 1)
    rs_hop(1, 3, 1, 3)
    rs_final(1, 1)
    rs_hop(1, 3, 0, 2)
    rs_hop(0, 3, 1, 2)
    rs_final(1, 0)
    rs_hop(0, 3, 0, 1)
    rs_hop(1, 3, 1, 2)
    rs_final(1, 2)
    rs_hop(0, 3, 1, 1)
    rs_hop(1, 3, 0, 1)
    rs_hop(1, 3, 1, 1)
    rs_final(0, 3)
    rs_final(1, 3)

    for c in sent:
        c.wait_send()
    for j, g in crossing:
        x_finish(j, g)


def body(gate_pre, up_pre, down_weight):
    hmat = jnp.asarray(np.kron(paley_matrix(), sylvester(32)), BF)
    dma = pltpu.SemaphoreType.DMA
    any_spec = pl.BlockSpec(memory_space=pl.ANY)
    return pl.pallas_call(
        functools.partial(kernel, 1.0 / math.sqrt(16 * KL)),
        out_shape=jax.ShapeDtypeStruct((TOKENS, 2 * CW), BF),
        in_specs=[any_spec] * 4,
        out_specs=pl.BlockSpec(memory_space=pltpu.VMEM),
        scratch_shapes=[
            pltpu.VMEM((KL, TOKENS), BF),
            pltpu.VMEM((KL, TOKENS), BF),
            pltpu.VMEM((KL, KL), BF),
            pltpu.VMEM((2, TOKENS, KL), BF),
            pltpu.VMEM((TOKENS, 2 * KL), BF),
            pltpu.VMEM((2, NZ, KB, CW), BF),
            pltpu.VMEM((2, NZ, KB, CW), BF),
            pltpu.VMEM((2, KB, NZ * CW), BF),
            pltpu.VMEM((2, 2 * KL, NZ * CW), BF),
            pltpu.VMEM((2, TOKENS, NZ * CW), F32),
            pltpu.VMEM((2 * NQ, 2, 4, TQ, CW), BF),
            pltpu.VMEM((2 * NQ, 2, 4, TQ, CW), BF),
            dma((5,)),
            dma((2, NZ)), dma((2, NZ)),
            dma((2, NZ)), dma((2, NZ)),
            dma((2, NG, 2)), dma((2, NG, 2)),
            dma((2, NG, 4)), dma((2, NG, 4)),
            dma((2, NG, 4)), dma((2, NG, 4)),
            dma((TOKENS // HX,)), dma((TOKENS // HX,)),
            dma((2 * NQ, 2, 4)), dma((2 * NQ, 2, 4)),
        ],
        compiler_params=pltpu.CompilerParams(
            collective_id=0, has_side_effects=True, vmem_limit_bytes=56 << 20),
        name=NAME,
    )(gate_pre.reshape(KL, TOKENS), up_pre.reshape(KL, TOKENS),
      down_weight.reshape(KL, 16 * 2 * CW), hmat).T


def solution(mesh):
    in_specs = (P(None, "tensor", "dp"), P(None, "tensor", "dp"), P(None, "tensor", None))
    out_specs = P("tensor", "dp")
    return jax.shard_map(body, mesh=mesh, in_specs=in_specs, out_specs=out_specs, check_vma=False)
```
